32 devices in a mesh: dp: 4 (over z), expert: 8 (over y, x, core).
Axes of the slice: x: 2, y: 2, z: 4, core: 2. Of those that a mesh axis runs over, the one named last changes fastest.
Arguments:
- attn_out: bfloat16 [2048, 4096], P('dp', 'expert'), may hold values from -6 to 6
- out_weight: bfloat16 [4096, 2880], P('expert'), may hold values from -0.09375 to 0.09375
- out_bias: float32 [2880], replicated, may hold values from -3 to 3
- residual_in: bfloat16 [2048, 2880], P(('dp', 'expert')), may hold values from -6 to 6
- norm_gain: float32 [2880], replicated, may hold values from 0.25 to 1.75
- router_weight: bfloat16 [2880, 8], replicated, may hold values from -0.109375 to 0.109375
- router_bias: float32 [8], replicated, may hold values from -1 to 332
- expert_ids: int32 [2048, 4], P(('dp', 'expert')), may hold values from 0 to 7, all different within a row; in each aligned block of 64 rows (0 to 63, 64 to 127, ...) at most 64 rows name the same one
- filled_rows: int32 [32], P(('dp', 'expert')), may hold values from 1 to 64, as said below
- gate_up: bfloat16 [8, 2, 1440, 2880], P('expert', None, 'dp'), may hold values from -0.33398438 to 0.33398438
- gate_up_bias: float32 [8, 2, 1440], P('expert'), may hold values from -3 to 3
- down_weight: bfloat16 [8, 1440, 2880], P('expert', 'dp'), may hold values from -0.04736328 to 0.04736328
- down_bias: float32 [8, 2880], P('expert'), may hold values from -2 to 2
- next_gain: float32 [2880], replicated, may hold values from 0.25 to 1.75
Outputs:
- stream: bfloat16 [2048, 2880], P(('dp', 'expert'))
- normed_next: bfloat16 [2048, 2880], P(('dp', 'expert'))
The draws below stay inside these ranges and needn't reach their ends.
Inputs may be any that keep to these rules, and one draw needn't show every extreme that they name: `expert_ids`: within each device's 64 rows (aligned blocks) no expert is named by more than 64 rows, a bound that some block reaches. `filled_rows`: some block is full.
All inputs are finite; a program needn't handle non-finite values.
Results may differ from the reference program's by a relative error of at most 0.015.
Values may be sent and summed in bfloat16 or wider, within the bound.
A program may use at most 192 MiB of HBM per device.

```python
import math
import jax
import jax.numpy as jnp
import numpy as np
from jax import lax

D = 2880
ATTN = 4096
TOP = 4
FFW = 1440
TOK_DEV = 64
EXPERTS = 8
CAP = 64
BLOCKS = 32
TOKENS = 2048
N_EXPERT = 8


def draw_router_bias(key, part):
    base = jax.random.uniform(key, (EXPERTS,), jnp.float32, -1.0, 1.0)
    return base


def draw_filled_rows(key, part):
    counts = jax.random.randint(jax.random.fold_in(key, 3), (BLOCKS,), 1, TOK_DEV + 1)
    spot = jax.random.randint(jax.random.fold_in(key, 5), (), 0, BLOCKS)
    return counts.at[spot].set(TOK_DEV).astype(jnp.int32)


def strengthened(values, key, source, target, shards_of, factor):
    owner, partner = [(jnp.arange(values.shape[position]) // (values.shape[position] // shards_of)).reshape([-1 if axis == position else 1 for axis in range(values.ndim)]) for position in (source, target)]
    chosen = jax.random.permutation(key, shards_of)[partner]
    strong = (owner == chosen) | (owner == (partner + shards_of // 2) % shards_of)
    return jnp.where(strong, factor * values, values)


def shard_levels(stream_key, dims, shards, low, top_value):
    level = 1.0
    for dim, blocks in shards:
        draws = jax.random.uniform(jax.random.fold_in(jax.random.fold_in(stream_key, 6), dim), (blocks,), jnp.float32, low / len(shards), top_value / len(shards))
        level = level * jnp.repeat(jnp.exp(draws), dims[dim] // blocks).reshape((-1,) + (1,) * (len(dims) - 1 - dim))
    return level


def shared_out(rng, own, number, rows, count, top, bound, lean):
    ranking = jax.random.permutation(rng, count)
    heavy_load, common = shares(count, rows * top, bound, lean, True), shares(count, rows * top, bound, lean, False)
    places = jnp.arange(count)

    def named(tallies, offset_by):
        used = int((tallies > 0).sum())
        fixed = max(1, used // 4)
        shifted = fixed + (places - fixed + offset_by * (used - fixed)) % max(1, count - fixed)
        return jnp.zeros((count,), jnp.int32).at[ranking[jnp.where(places < fixed, places, shifted)]].set(jnp.asarray(tallies, jnp.int32))

    tallies = jnp.where(number % 4 == 0, named(heavy_load, number // 4), named(common, number - number // 4 - 1))
    mixed = jax.random.permutation(jax.random.fold_in(own, 3), count)
    giver, receiver = mixed[0:count // 2 * 2:2], mixed[1:count // 2 * 2:2]
    margin = jnp.minimum(tallies[giver] - 1, bound - tallies[receiver]) // 2
    margin = jnp.where((giver == ranking[0]) | (receiver == ranking[0]) | (tallies[receiver] == 0), 0, jnp.maximum(margin, 0))
    shifted = jax.random.randint(jax.random.fold_in(own, 4), (count // 2,), 0, 1 << 20) % (margin + 1)
    tallies = tallies.at[giver].add(-shifted).at[receiver].add(shifted)
    items = jnp.searchsorted(jnp.cumsum(tallies), jnp.arange(rows * top), side="right").astype(jnp.int32)
    grid = items.reshape(top, rows).T
    grid = grid[jax.random.permutation(jax.random.fold_in(own, 1), rows)]
    offset_by = jax.random.randint(jax.random.fold_in(own, 2), (rows, 1), 0, top)
    return jnp.take_along_axis(grid, (jnp.arange(top)[None, :] + offset_by) % top, axis=1)


def shares(number_of, total, most, lean, full):
    loads = [(1 << 20) // math.isqrt(rank ** lean) + 1 for rank in range(1, number_of + 1)]
    largest = most if full else min(most, max(-(-total // number_of), total * loads[0] // sum(loads)))
    least = 1 if total - largest >= number_of - 1 else 0
    given, rest = [largest] + [least] * (number_of - 1), total - largest - least * (number_of - 1)
    while rest > 0:
        movable = [i for i in range(1, number_of) if given[i] < largest] or [i for i in range(1, number_of) if given[i] < most]
        pool, budget = sum([loads[i] for i in movable]), rest
        for i in movable:
            more = min(most - given[i], max(1, budget * loads[i] // pool), rest)
            given[i] = given[i] + more
            rest = rest - more
    return np.array(given)


def centred(rng, extent, deviation, bound, shards=(), kind=jnp.bfloat16):
    values = deviation * jax.random.normal(rng, extent, jnp.float32)
    if shards:
        values = values * shard_levels(rng, extent, shards, -0.22, 0.18)
    return jnp.clip(values, -bound, bound).astype(kind)


def heavy_noise(rng, dims, width, limit, cuts, heavy, held_as=jnp.bfloat16):
    entries = width * jax.random.normal(rng, dims, jnp.float32)
    if cuts:
        entries = entries * shard_levels(rng, dims, cuts, -0.22, 0.18)
    return jnp.clip(strengthened(entries, jax.random.fold_in(rng, 3), *heavy), -limit, limit).astype(held_as)


def setup_inputs(seed: int = 0) -> dict:
    splits = jax.random.split(jax.random.key(seed), 15)
    attn_out = heavy_noise(splits[0], (TOKENS, ATTN), 1.0, 6.0, ((0, 4), (1, 8)), (1, 0, 8, 2.0))
    out_weight = centred(splits[1], (ATTN, D), ATTN ** -0.5, 0.09375, ((0, 8),))
    out_bias = centred(splits[2], (D,), 0.5, 3.0, (), jnp.float32)
    residual_in = centred(splits[3], (TOKENS, D), 1.0, 6.0, ((0, 32),))
    norm_gain = jnp.clip(1.0 + 0.15 * jax.random.normal(splits[4], (D,), jnp.float32), 0.25, 1.75)
    router_weight = centred(splits[5], (D, EXPERTS), D ** -0.5, 0.109375)
    router_bias = draw_router_bias(jax.random.fold_in(splits[14], 71), 0)
    expert_ids_keys = jax.random.split(jax.random.fold_in(splits[7], 1), TOKENS // TOK_DEV)
    expert_ids_turns = jax.random.permutation(jax.random.fold_in(splits[7], 3), TOKENS // TOK_DEV)
    expert_ids = jax.vmap(lambda own, number: shared_out(jax.random.fold_in(splits[7], 2), own, number, TOK_DEV, EXPERTS, TOP, CAP, 2))(expert_ids_keys, expert_ids_turns).reshape((TOKENS, TOP))
    filled_rows = draw_filled_rows(jax.random.fold_in(splits[14], 71), 0)
    gate_up = centred(splits[9], (EXPERTS, 2, FFW, D), (3.0 * D ** -0.5), 0.33398438, ((0, 8), (2, 4)))
    gate_up_bias = centred(splits[10], (EXPERTS, 2, FFW), 0.5, 3.0, ((0, 8),), jnp.float32)
    down_weight = centred(splits[11], (EXPERTS, FFW, D), (0.3 * FFW ** -0.5), 0.04736328, ((0, 8), (1, 4)))
    down_bias = centred(splits[12], (EXPERTS, D), 0.3, 2.0, ((0, 8),), jnp.float32)
    next_gain = jnp.clip(1.0 + 0.15 * jax.random.normal(splits[13], (D,), jnp.float32), 0.25, 1.75)
    return dict(attn_out=attn_out, out_weight=out_weight, out_bias=out_bias, residual_in=residual_in, norm_gain=norm_gain, router_weight=router_weight, router_bias=router_bias, expert_ids=expert_ids, filled_rows=filled_rows, gate_up=gate_up, gate_up_bias=gate_up_bias, down_weight=down_weight, down_bias=down_bias, next_gain=next_gain)


EPS = 1e-05
LIMIT = 7.0
ALPHA = 1.702

def normalize(values, gain):
    return values * lax.rsqrt(lax.optimization_barrier(jnp.mean(values * values, axis=-1, keepdims=True)) + EPS) * gain

def activate(gate_part, up_part):
    gate_part = jnp.minimum(gate_part, LIMIT)
    up_part = jnp.clip(up_part, -LIMIT, LIMIT)
    return ((up_part + 1.0) * gate_part * jax.nn.sigmoid(ALPHA * gate_part)).astype(jnp.bfloat16)

def reference(attn_out, out_weight, out_bias, residual_in, norm_gain, router_weight, router_bias, expert_ids, filled_rows, gate_up, gate_up_bias, down_weight, down_bias, next_gain):
    head_width = ATTN // N_EXPERT
    attn_parts = attn_out.reshape(TOKENS, N_EXPERT, head_width).transpose(1, 0, 2)
    weight_parts = out_weight.reshape(N_EXPERT, head_width, D)

    def add_part(running, pair_in):
        partial_sum = jnp.dot(pair_in[0], pair_in[1], preferred_element_type=jnp.float32)
        rounded = lax.optimization_barrier(partial_sum.astype(jnp.bfloat16))
        return (running + rounded.astype(jnp.float32), None)
    summed, unused = lax.scan(add_part, jnp.zeros((TOKENS, D), jnp.float32), (attn_parts, weight_parts))
    hidden_state = residual_in.astype(jnp.float32) + summed + out_bias
    normed_in = normalize(hidden_state, norm_gain).astype(jnp.bfloat16)
    logits = jnp.dot(normed_in, router_weight, preferred_element_type=jnp.float32) + router_bias
    chosen = jnp.take_along_axis(logits, expert_ids, axis=1)
    route_probs = jax.nn.softmax(chosen, axis=-1)
    positions = jnp.arange(TOKENS, dtype=jnp.int32)
    live_rows = positions % TOK_DEV < filled_rows[positions // TOK_DEV]
    route_weights = route_probs * live_rows[:, None].astype(jnp.float32)
    flat_ids = expert_ids.reshape(-1)
    flat_weights = route_weights.reshape(-1)
    most_rows = BLOCKS * CAP

    def one_expert(running, expert_index):
        hit_mask = flat_ids == expert_index
        found_rows = jnp.nonzero(hit_mask, size=most_rows, fill_value=0)[0].astype(jnp.int32)
        valid_rows = jnp.arange(most_rows, dtype=jnp.int32) < jnp.sum(hit_mask.astype(jnp.int32))
        token_index = found_rows // TOP
        row_block = normed_in[token_index].astype(jnp.float32)
        pair_weights = gate_up[expert_index].astype(jnp.float32)
        gate_part = jnp.dot(row_block, pair_weights[0].T) + gate_up_bias[expert_index, 0]
        up_part = jnp.dot(row_block, pair_weights[1].T) + gate_up_bias[expert_index, 1]
        hidden = activate(gate_part, up_part)
        result = jnp.dot(hidden.astype(jnp.float32), down_weight[expert_index].astype(jnp.float32)) + down_bias[expert_index]
        result = result.astype(jnp.bfloat16)
        contrib = result.astype(jnp.float32) * flat_weights[found_rows][:, None]
        target = jnp.where(valid_rows, token_index, TOKENS)
        return (running.at[target].add(contrib, mode='drop'), None)
    mixture, unused = lax.scan(one_expert, jnp.zeros((TOKENS, D), jnp.float32), jnp.arange(EXPERTS, dtype=jnp.int32))
    stream_full = hidden_state + mixture
    return (stream_full.astype(jnp.bfloat16), normalize(stream_full, next_gain).astype(jnp.bfloat16))
```

```python
import functools

import jax
import jax.numpy as jnp
from jax import lax
from jax.experimental import pallas as pl
from jax.experimental.pallas import tpu as pltpu
from jax.sharding import PartitionSpec as P

EPS = 1e-05
LIMIT = 7.0
ALPHA = 1.702


def normalize(values, gain):
    return values * lax.rsqrt(jnp.mean(values * values, axis=-1, keepdims=True) + EPS) * gain


def activate(gate_part, up_part):
    gate_part = jnp.minimum(gate_part, LIMIT)
    up_part = jnp.clip(up_part, -LIMIT, LIMIT)
    return ((up_part + 1.0) * gate_part * jax.nn.sigmoid(ALPHA * gate_part)).astype(jnp.bfloat16)


def hidden_units(row_block, pair_weights, bias_part):
    numbers = (((1,), (1,)), ((), ()))
    gate_part = (
        lax.dot_general(row_block, pair_weights[0], numbers, preferred_element_type=jnp.float32)
        + bias_part[0]
    )
    up_part = (
        lax.dot_general(row_block, pair_weights[1], numbers, preferred_element_type=jnp.float32)
        + bias_part[1]
    )
    return activate(gate_part, up_part)


def routed_body(
    attn_out,
    out_weight,
    out_bias,
    residual_in,
    norm_gain,
    router_weight,
    router_bias,
    expert_ids,
    filled_rows,
    gate_up,
    gate_up_bias,
    down_weight,
    down_bias,
    next_gain,
):
    local_count = gate_up.shape[0]
    model_width = residual_in.shape[1]
    tok_rows = residual_in.shape[0]
    top_count = expert_ids.shape[1]
    experts_all = local_count * lax.axis_size("expert")
    capacity = 2 * tok_rows * top_count // experts_all
    row_block = attn_out
    summed = lax.psum_scatter(
        jnp.dot(row_block, out_weight, preferred_element_type=jnp.float32).astype(jnp.bfloat16),
        "expert",
        scatter_dimension=0,
        tiled=True,
    ).astype(jnp.float32)
    hidden_state = residual_in.astype(jnp.float32) + summed + out_bias
    normed_in = normalize(hidden_state, norm_gain).astype(jnp.bfloat16)
    logits = jnp.dot(normed_in, router_weight, preferred_element_type=jnp.float32) + router_bias
    chosen = jnp.take_along_axis(logits, expert_ids, axis=1)
    route_probs = jax.nn.softmax(chosen, axis=-1)
    live_rows = jnp.arange(tok_rows, dtype=jnp.int32) < filled_rows[0]
    route_weights = route_probs * live_rows[:, None].astype(jnp.float32)
    flat_ids = expert_ids.reshape(-1)
    onehot = (flat_ids[:, None] == jnp.arange(experts_all, dtype=jnp.int32)[None, :]).astype(
        jnp.int32
    )
    places = jnp.arange(flat_ids.shape[0], dtype=jnp.int32)
    earlier = (places[:, None] > places[None, :]).astype(jnp.bfloat16)
    before = jnp.dot(
        earlier, onehot.astype(jnp.bfloat16), preferred_element_type=jnp.float32
    ).astype(jnp.int32)
    slot_ids = flat_ids * capacity + jnp.sum(before * onehot, axis=1)
    placing = (
        jnp.arange(experts_all * capacity, dtype=jnp.int32)[:, None] == slot_ids[None, :]
    ).astype(jnp.bfloat16)
    repeated = jnp.repeat(normed_in, top_count, axis=0)
    outgoing = jnp.dot(placing, repeated, preferred_element_type=jnp.float32).astype(jnp.bfloat16)
    outgoing = outgoing.reshape(experts_all, capacity, model_width)
    arrived = lax.all_to_all(outgoing, "expert", split_axis=0, concat_axis=0, tiled=True)
    arrived = arrived.reshape(-1, local_count, capacity, model_width)
    row_block = arrived[:, 0].reshape(-1, model_width)
    bias_pair = gate_up_bias[0]
    hidden = hidden_units(
        row_block, lax.all_gather(gate_up[0], "dp", axis=1, tiled=True), bias_pair
    )
    summed_rows = jnp.dot(
        hidden,
        lax.all_gather(down_weight[0], "dp", axis=0, tiled=True),
        preferred_element_type=jnp.float32,
    )
    results = [(summed_rows + down_bias[0]).astype(jnp.bfloat16).reshape(-1, capacity, model_width)]
    answered = jnp.stack(results, axis=1).reshape(-1, capacity, model_width)
    returned = lax.all_to_all(answered, "expert", split_axis=0, concat_axis=0, tiled=True)
    returned = returned.reshape(experts_all * capacity, model_width)
    picked = returned[slot_ids].astype(jnp.float32).reshape(tok_rows, top_count, model_width)
    mixture = jnp.sum(picked * route_weights[:, :, None], axis=1)
    stream_full = hidden_state + mixture
    return (
        stream_full.astype(jnp.bfloat16),
        normalize(stream_full, next_gain).astype(jnp.bfloat16),
    )


def place():
    z, e = lax.axis_index("dp"), lax.axis_index("expert")
    y, x, core = e // 4, (e // 2) % 2, e % 2
    at = lambda yy, xx, cc: yy * 4 + xx * 2 + cc
    return dict(
        z=z, e=e, y=y, x=x, core=core,
        s=at(y, x, 1 - core), xn=at(y, 1 - x, core), yn=at(1 - y, x, core),
        dn=at(1 - y, 1 - x, core),
    )


def remote(src, dst, send_sem, recv_sem, device):
    return pltpu.make_async_remote_copy(
        src_ref=src, dst_ref=dst, send_sem=send_sem, recv_sem=recv_sem,
        device_id=device, device_id_type=pl.DeviceIdType.MESH,
    )


def greet(devices):
    barrier = pltpu.get_barrier_semaphore()
    for device in devices:
        pl.semaphore_signal(
            barrier, inc=1, device_id=device, device_id_type=pl.DeviceIdType.MESH
        )
    pl.semaphore_wait(barrier, len(devices))


class Plane:
    def __init__(self, here, parts, paired, from_x, from_y, last, send, recv, sent):
        self.here, self.parts, self.paired = here, parts, paired
        self.from_x, self.from_y, self.last = from_x, from_y, last
        self.send, self.recv, self.sent = send, recv, sent
        self.rows = parts.shape[3]
        self.low, self.high = pl.ds(0, self.rows // 2), pl.ds(self.rows // 2, self.rows // 2)

    def put(self, src, dst, lane, to):
        copy = remote(src, dst, self.send.at[lane], self.recv.at[lane], self.here[to])
        copy.start()
        self.sent.append(copy)

    def take(self, dst, lane, to):
        remote(dst, dst, self.send.at[lane], self.recv.at[lane], self.here[to]).wait_recv()

    def fill(self, values):
        for i in range(8):
            self.parts[i % 2, i // 4, (i // 2) % 2] = values[i * self.rows : (i + 1) * self.rows]
        self.put(self.parts.at[1 - self.here["core"]], self.paired, 0, "to_s")

    def join(self):
        core = self.here["core"]
        self.take(self.paired, 0, "to_s")

        @pl.loop(0, 4)
        def _(i):
            yy, xx = i // 2, i % 2
            self.parts[core, yy, xx] = self.parts[core, yy, xx] + self.paired[yy, xx]

    def first(self):
        core, x, y = self.here["core"], self.here["x"], self.here["y"]
        self.put(self.parts.at[core, :, 1 - x, self.low], self.from_x, 1, "to_x")
        self.put(self.parts.at[core, 1 - y, :, self.high], self.from_y, 2, "to_y")

    def second(self):
        core, x, y = self.here["core"], self.here["x"], self.here["y"]
        low, high = self.low, self.high
        self.take(self.from_x, 1, "to_x")
        self.parts[core, 1 - y, x, low] = self.parts[core, 1 - y, x, low] + self.from_x[1 - y]
        self.put(self.parts.at[core, 1 - y, x, low], self.last.at[low], 3, "to_y")
        self.take(self.from_y, 2, "to_y")
        self.parts[core, y, 1 - x, high] = self.parts[core, y, 1 - x, high] + self.from_y[1 - x]
        self.put(self.parts.at[core, y, 1 - x, high], self.last.at[high], 4, "to_x")

    def third(self):
        core, x, y = self.here["core"], self.here["x"], self.here["y"]
        self.take(self.last.at[self.low], 3, "to_y")
        self.take(self.last.at[self.high], 4, "to_x")
        own = self.parts[core, y, x].astype(jnp.float32) + self.last[...].astype(jnp.float32)
        more = jnp.concatenate(
            [self.from_x[y].astype(jnp.float32), self.from_y[x].astype(jnp.float32)], axis=0
        )
        return own + more


HALVES = 2


def layer_kernel(
    attn_all, out_all, residual_all, gate_up_all, down_all, ids, filled, router, router_bias,
    out_bias, norm_gain, next_gain, bias_all, down_bias,
    stream_out, next_out,
    attn, out_weight, residual, gu, dw, lsem, wide_router, bias_pair, hidden_state,
    proj_parts, proj_paired, proj_x, proj_y, proj_last, psend, precv,
    tok, gsend, grecv,
    parts, paired, from_x, from_y, last, corner_in, plane_in, far_out, far_in, rsend, rrecv,
):
    here = place()
    z, e, x, y, core = here["z"], here["e"], here["x"], here["y"], here["core"]
    xn, yn, dn = here["xn"], here["yn"], here["dn"]
    here["to_s"], here["to_x"], here["to_y"] = (z, here["s"]), (z, xn), (z, yn)
    to_s, to_x, to_y = here["to_s"], here["to_x"], here["to_y"]
    to_z = (None, (z + 1 - 2 * (z % 2), e), (3 - z, e), ((z + 2) % 4, e))
    loads = [
        pltpu.make_async_copy(src, dst, lsem.at[i])
        for i, (src, dst) in enumerate(
            (
                (out_all, out_weight), (attn_all, attn), (residual_all, residual),
                (gate_up_all, gu), (down_all, dw),
            )
        )
    ]
    for load in loads:
        load.start()
    greet([to_s, to_x, to_y, *to_z[1:]])
    rows = tok.shape[3]
    width = residual.shape[1]
    experts_all = router.shape[0]
    units = bias_pair.shape[1]
    low, high = pl.ds(0, rows // 2), pl.ds(rows // 2, rows // 2)
    sent = []
    proj = [
        Plane(
            here, proj_parts.at[h], proj_paired.at[h], proj_x.at[h], proj_y.at[h],
            proj_last.at[h], psend.at[h], precv.at[h], sent,
        )
        for h in range(HALVES)
    ]
    plane = {
        (k, h): Plane(
            here, parts.at[k, h], paired.at[k, h], from_x.at[k % 2, h], from_y.at[k % 2, h],
            last.at[k % 2, h], rsend.at[k, h], rrecv.at[k, h], sent,
        )
        for k in range(4)
        for h in range(HALVES)
    }

    def put(src, dst, k, h, lane, device):
        copy = remote(src, dst, gsend.at[k, h, lane], grecv.at[k, h, lane], device)
        copy.start()
        sent.append(copy)

    def take(dst, k, h, lane, device):
        remote(dst, dst, gsend.at[k, h, lane], grecv.at[k, h, lane], device).wait_recv()

    def multiply(h):
        block = attn[:, :, h * rows : (h + 1) * rows].reshape(8 * rows, attn.shape[3])
        proj[h].fill(
            lax.dot_general(
                block, out_weight[...], (((1,), (1,)), ((), ())),
                preferred_element_type=jnp.float32,
            ).astype(jnp.bfloat16)
        )

    def finish(h):
        span = slice(h * rows, (h + 1) * rows)
        total = residual[span].astype(jnp.float32) + proj[h].third() + out_bias[...]
        hidden_state[span] = total
        normed = normalize(total, norm_gain[...]).astype(jnp.bfloat16)
        tok[0, h, e, :, :width] = normed
        logits = lax.dot_general(
            normed, wide_router[...], (((1,), (1,)), ((), ())),
            preferred_element_type=jnp.float32,
        )
        lane = lax.broadcasted_iota(jnp.int32, logits.shape, 1) - 64
        row = lax.broadcasted_iota(jnp.int32, logits.shape, 0) + h * rows
        number = jnp.where(lane < experts_all, lane, lane - experts_all)
        valid = (lane >= 0) & (lane < 2 * experts_all)
        bias = jnp.zeros(logits.shape, jnp.float32)
        for j in range(experts_all):
            bias = jnp.where(number == j, router_bias[j], bias)
        named = ids[span, 0:1] == number
        for k in range(1, ids.shape[1]):
            named = named | (ids[span, k : k + 1] == number)
        named = named & valid
        logits = jnp.where(named, logits + bias, -jnp.inf)
        powers = jnp.exp(logits - jnp.max(logits, axis=1, keepdims=True))
        once = jnp.sum(jnp.where(lane < experts_all, powers, 0.0), axis=1, keepdims=True)
        weight = jnp.where(row < filled[0], powers / once, 0.0)
        coarse = weight.astype(jnp.bfloat16).astype(jnp.float32)
        packed = jnp.where(lane < experts_all, coarse, weight - coarse)
        tail = tok[0, h, e, :, tok.shape[4] - 128 :].astype(jnp.float32)
        tok[0, h, e, :, tok.shape[4] - 128 :] = jnp.where(lane < 0, tail, packed).astype(
            jnp.bfloat16
        )

    def enter(h):
        mine = tok.at[0, h, e]
        put(mine, mine, 0, h, 1, to_x)
        put(mine, mine, 0, h, 2, to_y)
        put(mine, mine, 0, h, 5, to_s)

    def enter_far(h):
        mine = tok.at[0, h, e]
        for k in (1, 2, 3):
            put(mine, tok.at[k, h, e], k, h, 0, to_z[k])

    def arrive(k, h):
        block = tok.at[k, h, e]
        take(block, k, h, 0, to_z[k])
        if k == 3:
            put(block, block, k, h, 1, to_x)
            put(block, block, k, h, 2, to_y)
        put(block, block, k, h, 5, to_s)

    def across(k, h):
        for lane, at, rest, onward in ((1, xn, low, to_y), (2, yn, high, to_x)):
            block = tok.at[k, h, at]
            take(block, k, h, lane, to_z[k] if k in (1, 2) else (to_x, to_y)[lane - 1])
            put(tok.at[k, h, at, rest], tok.at[k, h, at, rest], k, h, lane + 2, onward)
            if k == 0:
                for other in (1, 2):
                    put(block, tok.at[other, h, at], other, h, lane, to_z[other])
            put(block, block, k, h, lane + 5, to_s)

    def corner(k, h):
        take(tok.at[k, h, dn, low], k, h, 3, to_y)
        take(tok.at[k, h, dn, high], k, h, 4, to_x)
        put(tok.at[k, h, dn], tok.at[k, h, dn], k, h, 8, to_s)

    def compute(k, h):
        for lane, name in ((5, "e"), (6, "xn"), (7, "yn"), (8, "dn")):
            take(tok.at[k, h, here[name] + 1 - 2 * core], k, h, lane, to_s)
        values = tok[k, h, :, :, :width].reshape(8 * rows, width)
        hidden = hidden_units(values, (gu[0], gu[1]), (bias_pair[0:1], bias_pair[1:2]))
        part = jnp.dot(hidden, dw[...], preferred_element_type=jnp.float32)
        part = part + jnp.where(z == 0, down_bias[...], 0.0)
        tail = tok[k, h, :, :, tok.shape[4] - 128 :].reshape(8 * rows, 128)
        lane = lax.broadcasted_iota(jnp.int32, tail.shape, 1) - 64
        picked = (lane == e) | (lane == e + experts_all)
        share = jnp.sum(jnp.where(picked, tail.astype(jnp.float32), 0.0), axis=1, keepdims=True)
        plane[k, h].fill((part * share).astype(jnp.bfloat16))

    def join(k, h):
        part = plane[k, h]
        part.join()
        if k == 3:
            part.first()
        if k in (1, 2):
            arrives = corner_in.at[k - 1, h]
            part.put(part.parts.at[core, 1 - y, 1 - x, low], arrives.at[low], 3, "to_y")
            part.put(part.parts.at[core, 1 - y, 1 - x, high], arrives.at[high], 4, "to_x")
            here["far"] = to_z[k]
            part.put(part.parts.at[core, y, x], plane_in.at[k - 1, h, 0], 5, "far")

    def onward(k, h):
        part = plane[k, h]
        if k == 3:
            part.second()
            return
        arrives = corner_in.at[k - 1, h]
        here["far"] = to_z[k]
        part.take(arrives.at[low], 3, "to_y")
        part.parts[core, y, 1 - x, low] = part.parts[core, y, 1 - x, low] + arrives[low]
        part.put(part.parts.at[core, y, 1 - x], plane_in.at[k - 1, h, 1], 1, "far")
        part.take(arrives.at[high], 4, "to_x")
        part.parts[core, 1 - y, x, high] = part.parts[core, 1 - y, x, high] + arrives[high]
        part.put(part.parts.at[core, 1 - y, x], plane_in.at[k - 1, h, 2], 2, "far")

    def leave(h):
        part = plane[3, h]
        far_out[h] = part.third().astype(jnp.bfloat16)
        here["far"] = to_z[3]
        part.put(far_out.at[h], far_in.at[h], 5, "far")

    def merge(h):
        part = plane[0, h]
        for j, yy, xx in ((1, y, 1 - x), (2, 1 - y, x)):
            for k in (1, 2):
                here["far"] = to_z[k]
                plane[k, h].take(plane_in.at[k - 1, h, j], j, "far")
            part.parts[core, yy, xx] = (
                part.parts[core, yy, xx].astype(jnp.float32)
                + plane_in[0, h, j].astype(jnp.float32)
                + plane_in[1, h, j].astype(jnp.float32)
            ).astype(jnp.bfloat16)
        part.first()

    def final(h):
        total = plane[0, h].third()
        span = slice(h * rows, (h + 1) * rows)
        for k in (1, 2):
            here["far"] = to_z[k]
            plane[k, h].take(plane_in.at[k - 1, h, 0], 5, "far")
            total = total + plane_in[k - 1, h, 0].astype(jnp.float32)
        here["far"] = to_z[3]
        plane[3, h].take(far_in.at[h], 5, "far")
        total = hidden_state[span] + (total + far_in[h].astype(jnp.float32))
        stream_out[span] = total.astype(jnp.bfloat16)
        next_out[span] = normalize(total, next_gain[...]).astype(jnp.bfloat16)

    bias_pair[...] = sum(
        jnp.where(z == j, bias_all[:, j * units : (j + 1) * units], 0.0) for j in range(4)
    )
    twice = router[...].astype(jnp.float32)
    wide_router[64 : 64 + 2 * experts_all] = jnp.concatenate([twice, twice], axis=0).astype(
        jnp.bfloat16
    )
    loads[0].wait()
    loads[1].wait()
    multiply(0)
    multiply(1)
    for h in range(HALVES):
        proj[h].join()
        proj[h].first()
    for h in range(HALVES):
        proj[h].second()
    loads[2].wait()
    finish(0)
    enter(0)
    enter_far(0)
    finish(1)
    enter(1)
    loads[3].wait()
    loads[4].wait()
    for stage, k, h in STAGES:
        if stage in ("enter_far", "leave", "merge", "final"):
            {"enter_far": enter_far, "leave": leave, "merge": merge, "final": final}[stage](h)
        elif stage == "second":
            plane[k, h].second()
        else:
            {
                "across": across, "corner": corner, "arrive": arrive, "compute": compute,
                "join": join, "onward": onward,
            }[stage](k, h)
    for copy in sent:
        copy.wait_send()


STAGES = (
    ("across", 0, 0), ("enter_far", 0, 1), ("corner", 0, 0), ("arrive", 3, 0),
    ("compute", 0, 0), ("arrive", 1, 0), ("arrive", 2, 0), ("across", 0, 1), ("corner", 0, 1), ("across", 3, 0),
    ("compute", 0, 1), ("corner", 3, 0), ("across", 1, 0), ("across", 2, 0),
    ("compute", 3, 0), ("corner", 1, 0), ("corner", 2, 0), ("join", 0, 0), ("join", 3, 0), ("arrive", 3, 1),
    ("compute", 1, 0), ("join", 0, 1), ("onward", 3, 0),
    ("compute", 2, 0), ("join", 1, 0), ("arrive", 1, 1), ("arrive", 2, 1), ("across", 3, 1), ("leave", 0, 0), ("join", 2, 0), ("corner", 3, 1), ("onward", 1, 0), ("onward", 2, 0),
    ("compute", 3, 1), ("across", 1, 1), ("across", 2, 1), ("corner", 1, 1), ("corner", 2, 1), ("join", 3, 1),
    ("compute", 1, 1), ("onward", 3, 1),
    ("compute", 2, 1), ("join", 1, 1), ("join", 2, 1), ("leave", 0, 1), ("onward", 1, 1), ("onward", 2, 1),
    ("merge", 0, 0), ("second", 0, 0), ("merge", 0, 1), ("second", 0, 1), ("final", 0, 0), ("final", 0, 1),
)


def layer(
    attn_out, out_weight, residual_in, gate_up, down, ids, filled, router, router_bias,
    out_bias, norm_gain, next_gain, bias_all, down_bias,
):
    tokens, features = attn_out.shape
    block_rows, width = residual_in.shape
    rows = block_rows // HALVES
    wide = -(-width // 128) * 128
    bf16, f32 = jnp.bfloat16, jnp.float32
    vmem = pl.BlockSpec(memory_space=pltpu.VMEM)
    smem = pl.BlockSpec(memory_space=pltpu.SMEM)
    anywhere = pl.BlockSpec(memory_space=pl.ANY)
    attn = attn_out.reshape(4, 2, block_rows, features)
    out_rows = out_weight.T
    dma = pltpu.SemaphoreType.DMA
    return pl.pallas_call(
        layer_kernel,
        out_shape=[jax.ShapeDtypeStruct((block_rows, width), bf16)] * 2,
        in_specs=[anywhere] * 5 + [vmem, smem, vmem, smem] + [vmem] * 5,
        out_specs=[vmem, vmem],
        scratch_shapes=[
            pltpu.VMEM(attn.shape, bf16),
            pltpu.VMEM(out_rows.shape, bf16),
            pltpu.VMEM(residual_in.shape, bf16),
            pltpu.VMEM(gate_up.shape, bf16),
            pltpu.VMEM(down.shape, bf16),
            dma((5,)),
            pltpu.VMEM((128, width), bf16),
            pltpu.VMEM(gate_up.shape[:2], f32),
            pltpu.VMEM((block_rows, width), f32),
            pltpu.VMEM((HALVES, 2, 2, 2, rows, width), bf16),
            pltpu.VMEM((HALVES, 2, 2, rows, width), bf16),
            pltpu.VMEM((HALVES, 2, rows // 2, width), bf16),
            pltpu.VMEM((HALVES, 2, rows // 2, width), bf16),
            pltpu.VMEM((HALVES, rows, width), bf16),
            dma((HALVES, 5)),
            dma((HALVES, 5)),
            pltpu.VMEM((4, HALVES, 8, rows, wide), bf16),
            dma((4, HALVES, 9)),
            dma((4, HALVES, 9)),
            pltpu.VMEM((4, HALVES, 2, 2, 2, rows, width), bf16),
            pltpu.VMEM((4, HALVES, 2, 2, rows, width), bf16),
            pltpu.VMEM((2, HALVES, 2, rows // 2, width), bf16),
            pltpu.VMEM((2, HALVES, 2, rows // 2, width), bf16),
            pltpu.VMEM((2, HALVES, rows, width), bf16),
            pltpu.VMEM((2, HALVES, rows, width), bf16),
            pltpu.VMEM((2, HALVES, 3, rows, width), bf16),
            pltpu.VMEM((HALVES, rows, width), bf16),
            pltpu.VMEM((HALVES, rows, width), bf16),
            dma((4, HALVES, 6)),
            dma((4, HALVES, 6)),
        ],
        compiler_params=pltpu.CompilerParams(
            collective_id=0, has_side_effects=True, vmem_limit_bytes=60 * 1024 * 1024
        ),
    )(
        attn, out_rows, residual_in, gate_up, down, ids, filled, router, router_bias,
        out_bias, norm_gain, next_gain, bias_all, down_bias,
    )


def dense_body(
    attn_out,
    out_weight,
    out_bias,
    residual_in,
    norm_gain,
    router_weight,
    router_bias,
    expert_ids,
    filled_rows,
    gate_up,
    gate_up_bias,
    down_weight,
    down_bias,
    next_gain,
):
    return tuple(
        layer(
            attn_out, out_weight, residual_in, gate_up[0], down_weight[0], expert_ids,
            filled_rows, router_weight.T, router_bias, out_bias[None], norm_gain[None],
            next_gain[None], gate_up_bias[0], down_bias,
        )
    )


def body(*arrays):
    residual_in, gate_up, down_weight = arrays[3], arrays[9], arrays[11]
    dp_size, expert_size = lax.axis_size("dp"), lax.axis_size("expert")
    token_rows = residual_in.shape[0] * dp_size * expert_size
    weight_rows = dp_size * (2 * gate_up.shape[2] + down_weight.shape[1])
    if gate_up.shape[0] == 1 and expert_size == 8 and dp_size == 4 and 2 * token_rows <= weight_rows:
        return dense_body(*arrays)
    return routed_body(*arrays)


def solution(mesh):
    return jax.shard_map(
        body,
        mesh=mesh,
        in_specs=(
            P("dp", "expert"),
            P("expert", None),
            P(),
            P(("dp", "expert"), None),
            P(),
            P(),
            P(),
            P(("dp", "expert"), None),
            P(("dp", "expert")),
            P("expert", None, "dp", None),
            P("expert", None, None),
            P("expert", "dp", None),
            P("expert", None),
            P(),
        ),
        out_specs=(P(("dp", "expert"), None), P(("dp", "expert"), None)),
        check_vma=False,
    )
```

```python
import functools

import jax
import jax.numpy as jnp
from jax import lax
from jax.experimental import pallas as pl
from jax.experimental.pallas import tpu as pltpu
from jax.sharding import PartitionSpec as P

EPS = 1e-05
LIMIT = 7.0
ALPHA = 1.702


def normalize(values, gain):
    return values * lax.rsqrt(jnp.mean(values * values, axis=-1, keepdims=True) + EPS) * gain


def activate(gate_part, up_part):
    gate_part = jnp.minimum(gate_part, LIMIT)
    up_part = jnp.clip(up_part, -LIMIT, LIMIT)
    return ((up_part + 1.0) * gate_part * jax.nn.sigmoid(ALPHA * gate_part)).astype(jnp.bfloat16)


def hidden_units(row_block, pair_weights, bias_part):
    numbers = (((1,), (1,)), ((), ()))
    gate_part = (
        lax.dot_general(row_block, pair_weights[0], numbers, preferred_element_type=jnp.float32)
        + bias_part[0]
    )
    up_part = (
        lax.dot_general(row_block, pair_weights[1], numbers, preferred_element_type=jnp.float32)
        + bias_part[1]
    )
    return activate(gate_part, up_part)


def routed_body(
    attn_out,
    out_weight,
    out_bias,
    residual_in,
    norm_gain,
    router_weight,
    router_bias,
    expert_ids,
    filled_rows,
    gate_up,
    gate_up_bias,
    down_weight,
    down_bias,
    next_gain,
):
    local_count = gate_up.shape[0]
    model_width = residual_in.shape[1]
    tok_rows = residual_in.shape[0]
    top_count = expert_ids.shape[1]
    experts_all = local_count * lax.axis_size("expert")
    capacity = 2 * tok_rows * top_count // experts_all
    row_block = attn_out
    summed = lax.psum_scatter(
        jnp.dot(row_block, out_weight, preferred_element_type=jnp.float32).astype(jnp.bfloat16),
        "expert",
        scatter_dimension=0,
        tiled=True,
    ).astype(jnp.float32)
    hidden_state = residual_in.astype(jnp.float32) + summed + out_bias
    normed_in = normalize(hidden_state, norm_gain).astype(jnp.bfloat16)
    logits = jnp.dot(normed_in, router_weight, preferred_element_type=jnp.float32) + router_bias
    chosen = jnp.take_along_axis(logits, expert_ids, axis=1)
    route_probs = jax.nn.softmax(chosen, axis=-1)
    live_rows = jnp.arange(tok_rows, dtype=jnp.int32) < filled_rows[0]
    route_weights = route_probs * live_rows[:, None].astype(jnp.float32)
    flat_ids = expert_ids.reshape(-1)
    onehot = (flat_ids[:, None] == jnp.arange(experts_all, dtype=jnp.int32)[None, :]).astype(
        jnp.int32
    )
    places = jnp.arange(flat_ids.shape[0], dtype=jnp.int32)
    earlier = (places[:, None] > places[None, :]).astype(jnp.bfloat16)
    before = jnp.dot(
        earlier, onehot.astype(jnp.bfloat16), preferred_element_type=jnp.float32
    ).astype(jnp.int32)
    slot_ids = flat_ids * capacity + jnp.sum(before * onehot, axis=1)
    placing = (
        jnp.arange(experts_all * capacity, dtype=jnp.int32)[:, None] == slot_ids[None, :]
    ).astype(jnp.bfloat16)
    repeated = jnp.repeat(normed_in, top_count, axis=0)
    outgoing = jnp.dot(placing, repeated, preferred_element_type=jnp.float32).astype(jnp.bfloat16)
    outgoing = outgoing.reshape(experts_all, capacity, model_width)
    arrived = lax.all_to_all(outgoing, "expert", split_axis=0, concat_axis=0, tiled=True)
    arrived = arrived.reshape(-1, local_count, capacity, model_width)
    row_block = arrived[:, 0].reshape(-1, model_width)
    bias_pair = gate_up_bias[0]
    hidden = hidden_units(
        row_block, lax.all_gather(gate_up[0], "dp", axis=1, tiled=True), bias_pair
    )
    summed_rows = jnp.dot(
        hidden,
        lax.all_gather(down_weight[0], "dp", axis=0, tiled=True),
        preferred_element_type=jnp.float32,
    )
    results = [(summed_rows + down_bias[0]).astype(jnp.bfloat16).reshape(-1, capacity, model_width)]
    answered = jnp.stack(results, axis=1).reshape(-1, capacity, model_width)
    returned = lax.all_to_all(answered, "expert", split_axis=0, concat_axis=0, tiled=True)
    returned = returned.reshape(experts_all * capacity, model_width)
    picked = returned[slot_ids].astype(jnp.float32).reshape(tok_rows, top_count, model_width)
    mixture = jnp.sum(picked * route_weights[:, :, None], axis=1)
    stream_full = hidden_state + mixture
    return (
        stream_full.astype(jnp.bfloat16),
        normalize(stream_full, next_gain).astype(jnp.bfloat16),
    )


def place():
    z, e = lax.axis_index("dp"), lax.axis_index("expert")
    y, x, core = e // 4, (e // 2) % 2, e % 2
    at = lambda yy, xx, cc: yy * 4 + xx * 2 + cc
    return dict(
        z=z, e=e, y=y, x=x, core=core,
        s=at(y, x, 1 - core), xn=at(y, 1 - x, core), yn=at(1 - y, x, core),
        dn=at(1 - y, 1 - x, core),
    )


def remote(src, dst, send_sem, recv_sem, device):
    return pltpu.make_async_remote_copy(
        src_ref=src, dst_ref=dst, send_sem=send_sem, recv_sem=recv_sem,
        device_id=device, device_id_type=pl.DeviceIdType.MESH,
    )


def greet(devices):
    barrier = pltpu.get_barrier_semaphore()
    for device in devices:
        pl.semaphore_signal(
            barrier, inc=1, device_id=device, device_id_type=pl.DeviceIdType.MESH
        )
    pl.semaphore_wait(barrier, len(devices))


class Plane:
    def __init__(self, here, parts, paired, from_x, from_y, last, send, recv, sent):
        self.here, self.parts, self.paired = here, parts, paired
        self.from_x, self.from_y, self.last = from_x, from_y, last
        self.send, self.recv, self.sent = send, recv, sent
        self.rows = parts.shape[3]
        self.low, self.high = pl.ds(0, self.rows // 2), pl.ds(self.rows // 2, self.rows // 2)

    def put(self, src, dst, lane, to):
        copy = remote(src, dst, self.send.at[lane], self.recv.at[lane], self.here[to])
        copy.start()
        self.sent.append(copy)

    def take(self, dst, lane, to):
        remote(dst, dst, self.send.at[lane], self.recv.at[lane], self.here[to]).wait_recv()

    def fill(self, values):
        for i in range(8):
            self.parts[i % 2, i // 4, (i // 2) % 2] = values[i * self.rows : (i + 1) * self.rows]
        self.put(self.parts.at[1 - self.here["core"]], self.paired, 0, "to_s")

    def join(self):
        core = self.here["core"]
        self.take(self.paired, 0, "to_s")

        @pl.loop(0, 4)
        def _(i):
            yy, xx = i // 2, i % 2
            self.parts[core, yy, xx] = self.parts[core, yy, xx] + self.paired[yy, xx]

    def first(self):
        core, x, y = self.here["core"], self.here["x"], self.here["y"]
        self.put(self.parts.at[core, :, 1 - x, self.low], self.from_x, 1, "to_x")
        self.put(self.parts.at[core, 1 - y, :, self.high], self.from_y, 2, "to_y")

    def second(self):
        core, x, y = self.here["core"], self.here["x"], self.here["y"]
        low, high = self.low, self.high
        self.take(self.from_x, 1, "to_x")
        self.parts[core, 1 - y, x, low] = self.parts[core, 1 - y, x, low] + self.from_x[1 - y]
        self.put(self.parts.at[core, 1 - y, x, low], self.last.at[low], 3, "to_y")
        self.take(self.from_y, 2, "to_y")
        self.parts[core, y, 1 - x, high] = self.parts[core, y, 1 - x, high] + self.from_y[1 - x]
        self.put(self.parts.at[core, y, 1 - x, high], self.last.at[high], 4, "to_x")

    def third(self):
        core, x, y = self.here["core"], self.here["x"], self.here["y"]
        self.take(self.last.at[self.low], 3, "to_y")
        self.take(self.last.at[self.high], 4, "to_x")
        own = self.parts[core, y, x].astype(jnp.float32) + self.last[...].astype(jnp.float32)
        more = jnp.concatenate(
            [self.from_x[y].astype(jnp.float32), self.from_y[x].astype(jnp.float32)], axis=0
        )
        return own + more


HALVES = 2


def layer_kernel(
    attn_all, out_all, residual_all, gate_up_all, down_all, ids, filled, router, router_bias,
    out_bias, norm_gain, next_gain, bias_all, down_bias,
    stream_out, next_out,
    attn, out_weight, residual, gu, dw, lsem, wide_router, bias_pair, names, hidden_state,
    proj_parts, proj_paired, proj_x, proj_y, proj_last, psend, precv,
    tok, gsend, grecv,
    parts, paired, from_x, from_y, last, near_x, near_y, corner_in, far_out, far_in, rsend, rrecv,
):
    here = place()
    z, e, x, y, core = here["z"], here["e"], here["x"], here["y"], here["core"]
    xn, yn, dn = here["xn"], here["yn"], here["dn"]
    here["to_s"], here["to_x"], here["to_y"] = (z, here["s"]), (z, xn), (z, yn)
    here["to_1"] = (z + 1 - 2 * (z % 2), e)
    to_s, to_x, to_y = here["to_s"], here["to_x"], here["to_y"]
    to_z = (None, (z + 1 - 2 * (z % 2), e), ((z + 2) % 4, e), (3 - z, e))
    loads = [
        pltpu.make_async_copy(src, dst, lsem.at[i])
        for i, (src, dst) in enumerate(
            (
                (out_all, out_weight), (attn_all, attn), (residual_all, residual),
                (gate_up_all, gu), (down_all, dw),
            )
        )
    ]
    for load in loads[:3]:
        load.start()
    greet([to_s, to_x, to_y, *to_z[1:]])
    rows = tok.shape[3]
    width = residual.shape[1]
    experts_all = router.shape[0]
    units = bias_pair.shape[1]
    low, high = pl.ds(0, rows // 2), pl.ds(rows // 2, rows // 2)
    sent = []
    proj = [
        Plane(
            here, proj_parts.at[h], proj_paired.at[h], proj_x.at[h], proj_y.at[h],
            proj_last.at[h], psend.at[h], precv.at[h], sent,
        )
        for h in range(HALVES)
    ]
    plane = {
        (k, h): Plane(
            here, parts.at[k, h], paired.at[k, h], from_x.at[k // 2, h], from_y.at[k // 2, h],
            last.at[k // 2, h], rsend.at[k, h], rrecv.at[k, h], sent,
        )
        for k in range(4)
        for h in range(HALVES)
    }

    def put(src, dst, k, h, lane, device):
        copy = remote(src, dst, gsend.at[k, h, lane], grecv.at[k, h, lane], device)
        copy.start()
        sent.append(copy)

    def take(dst, k, h, lane, device):
        remote(dst, dst, gsend.at[k, h, lane], grecv.at[k, h, lane], device).wait_recv()

    def multiply(h):
        block = attn[:, :, h * rows : (h + 1) * rows].reshape(8 * rows, attn.shape[3])
        proj[h].fill(
            lax.dot_general(
                block, out_weight[...], (((1,), (1,)), ((), ())),
                preferred_element_type=jnp.float32,
            ).astype(jnp.bfloat16)
        )

    def finish(h):
        span = slice(h * rows, (h + 1) * rows)
        total = residual[span].astype(jnp.float32) + proj[h].third() + out_bias[...][None]
        hidden_state[span] = total
        normed = normalize(total, norm_gain[...][None]).astype(jnp.bfloat16)
        tok[0, h, e, :, :width] = normed
        logits = lax.dot_general(
            normed, wide_router[...], (((1,), (1,)), ((), ())),
            preferred_element_type=jnp.float32,
        )
        lane = lax.broadcasted_iota(jnp.int32, logits.shape, 1) - 64
        row = lax.broadcasted_iota(jnp.int32, logits.shape, 0) + h * rows
        bias = jnp.zeros((1, logits.shape[1]), jnp.float32)
        for j in range(experts_all):
            bias = jnp.where((lane[:1] == j) | (lane[:1] == j + experts_all), router_bias[j], bias)
        named = names[span] > 0.5
        logits = jnp.where(named, logits + bias, -jnp.inf)
        powers = jnp.exp(logits - jnp.max(logits, axis=1, keepdims=True))
        once = jnp.sum(jnp.where(lane < experts_all, powers, 0.0), axis=1, keepdims=True)
        weight = jnp.where(row < filled[0], powers / once, 0.0)
        coarse = weight.astype(jnp.bfloat16).astype(jnp.float32)
        packed = jnp.where(lane < experts_all, coarse, weight - coarse)
        tail = tok[0, h, e, :, tok.shape[4] - 128 :].astype(jnp.float32)
        tok[0, h, e, :, tok.shape[4] - 128 :] = jnp.where(lane < 0, tail, packed).astype(
            jnp.bfloat16
        )

    def enter(h):
        mine = tok.at[0, h, e]
        put(mine, mine, 0, h, 1, to_x)
        put(mine, mine, 0, h, 2, to_y)
        put(mine, mine, 0, h, 5, to_s)

    def enter_far(k, h):
        put(tok.at[0, h, e], tok.at[k, h, e], k, h, 0, to_z[k])

    def arrive(k, h):
        block = tok.at[k, h, e]
        take(block, k, h, 0, to_z[k])
        put(block, block, k, h, 1, to_x)
        put(block, block, k, h, 2, to_y)
        put(block, block, k, h, 5, to_s)

    def across(k, h):
        for lane, at, rest, source, onward in ((1, xn, low, to_x, to_y), (2, yn, high, to_y, to_x)):
            block = tok.at[k, h, at]
            take(block, k, h, lane, source)
            if k % 2 == 0:
                put(tok.at[k, h, at, rest], tok.at[k, h, at, rest], k, h, lane + 2, onward)
            put(block, block, k, h, lane + 5, to_s)

    def corner(k, h):
        block = tok.at[k, h, dn]
        if k % 2 == 0:
            take(tok.at[k, h, dn, low], k, h, 3, to_y)
            take(tok.at[k, h, dn, high], k, h, 4, to_x)
            put(block, tok.at[k + 1, h, dn], k + 1, h, 3, to_z[1])
        else:
            take(block, k, h, 3, to_z[1])
        put(block, block, k, h, 8, to_s)

    def compute(k, h):
        for lane, name in ((5, "e"), (6, "xn"), (7, "yn"), (8, "dn")):
            take(tok.at[k, h, here[name] + 1 - 2 * core], k, h, lane, to_s)
        values = tok[k, h, :, :, :width].reshape(8 * rows, width)
        hidden = hidden_units(values, (gu[0], gu[1]), (bias_pair[0:1], bias_pair[1:2]))
        part = jnp.dot(hidden, dw[...], preferred_element_type=jnp.float32)
        part = part + jnp.where(z == 0, down_bias[...], 0.0)
        tail = tok[k, h, :, :, tok.shape[4] - 128 :].reshape(8 * rows, 128)
        lane = lax.broadcasted_iota(jnp.int32, tail.shape, 1) - 64
        picked = (lane == e) | (lane == e + experts_all)
        share = jnp.sum(jnp.where(picked, tail.astype(jnp.float32), 0.0), axis=1, keepdims=True)
        plane[k, h].fill((part * share).astype(jnp.bfloat16))

    def join(k, h):
        part = plane[k, h]
        part.join()
        if k % 2 == 1:
            part.put(part.parts.at[core, 1 - y, 1 - x], corner_in.at[k // 2, h], 3, "to_1")
            part.put(part.parts.at[core, y, 1 - x], near_x.at[k // 2, h], 1, "to_x")
            part.put(part.parts.at[core, 1 - y, x], near_y.at[k // 2, h], 2, "to_y")

    def first(k, h):
        part = plane[k, h]
        plane[k + 1, h].take(corner_in.at[k // 2, h], 3, "to_1")
        part.parts[core, 1 - y, 1 - x] = part.parts[core, 1 - y, 1 - x] + corner_in[k // 2, h]
        part.first()

    def gathered(k, h):
        part = plane[k, h]
        if k % 2 == 0:
            return part.third()
        part.take(near_x.at[k // 2, h], 1, "to_x")
        part.take(near_y.at[k // 2, h], 2, "to_y")
        return (
            part.parts[core, y, x].astype(jnp.float32)
            + near_x[k // 2, h].astype(jnp.float32)
            + near_y[k // 2, h].astype(jnp.float32)
        )

    def leave(k, h):
        far_out[k - 1, h] = gathered(k, h).astype(jnp.bfloat16)
        here["far"] = to_z[k]
        plane[k, h].put(far_out.at[k - 1, h], far_in.at[k - 1, h], 5, "far")

    def final(h):
        total = gathered(0, h)
        span = slice(h * rows, (h + 1) * rows)
        for k in (1, 2, 3):
            here["far"] = to_z[k]
            plane[k, h].take(far_in.at[k - 1, h], 5, "far")
            total = total + far_in[k - 1, h].astype(jnp.float32)
        total = hidden_state[span] + total
        stream_out[span] = total.astype(jnp.bfloat16)
        next_out[span] = normalize(total, next_gain[...][None]).astype(jnp.bfloat16)

    bias_pair[...] = sum(
        jnp.where(z == j, bias_all[:, j * units : (j + 1) * units], 0.0) for j in range(4)
    )
    twice = router[...].astype(jnp.float32)
    wide_router[64 : 64 + 2 * experts_all] = jnp.concatenate([twice, twice], axis=0).astype(
        jnp.bfloat16
    )
    expert = lax.broadcasted_iota(jnp.int32, (experts_all, ids.shape[1]), 0)
    hits = sum(jnp.where(ids[k : k + 1] == expert, 1.0, 0.0) for k in range(ids.shape[0]))
    expert = lax.broadcasted_iota(jnp.int32, (experts_all, 128), 0)
    lane = lax.broadcasted_iota(jnp.int32, (experts_all, 128), 1) - 64
    spread = jnp.where((lane == expert) | (lane == expert + experts_all), 1.0, 0.0)
    names[...] = lax.dot_general(
        hits.astype(jnp.bfloat16), spread.astype(jnp.bfloat16), (((0,), (0,)), ((), ())),
        preferred_element_type=jnp.float32,
    )
    loads[0].wait()
    loads[1].wait()
    for load in loads[3:]:
        load.start()
    loads[2].wait()
    stages = dict(
        multiply=lambda k, h: multiply(h), pair=lambda k, h: proj[h].join(),
        proj1=lambda k, h: proj[h].first(), proj2=lambda k, h: proj[h].second(),
        finish=lambda k, h: finish(h), enter=lambda k, h: enter(h), far=enter_far,
        arrive=arrive, across=across, corner=corner, compute=compute, join=join, first=first,
        second=lambda k, h: plane[k, h].second(), leave=leave,
        final=lambda k, h: final(h),
    )
    loaded = False
    for stage, k, h in STAGES:
        if stage == "compute" and not loaded:
            loads[3].wait()
            loads[4].wait()
            loaded = True
        stages[stage](k, h)
    for copy in sent:
        copy.wait_send()


STAGES = (
    ("multiply", 0, 0), ("multiply", 0, 1), ("pair", 0, 0), ("proj1", 0, 0),
    ("proj2", 0, 0), ("pair", 0, 1), ("proj1", 0, 1), ("finish", 0, 0),
    ("enter", 0, 0), ("far", 2, 0), ("far", 1, 0), ("across", 0, 0),
    ("far", 3, 0), ("corner", 0, 0), ("proj2", 0, 1), ("arrive", 1, 0),
    ("finish", 0, 1), ("far", 2, 1), ("far", 1, 1), ("across", 1, 0),
    ("arrive", 2, 0), ("corner", 1, 0), ("enter", 0, 1), ("compute", 0, 0),
    ("across", 2, 0), ("arrive", 2, 1), ("corner", 2, 0), ("arrive", 3, 0),
    ("far", 3, 1), ("across", 0, 1), ("join", 0, 0), ("compute", 1, 0),
    ("across", 2, 1), ("across", 3, 0), ("corner", 3, 0), ("join", 1, 0),
    ("corner", 2, 1), ("arrive", 3, 1), ("compute", 3, 0), ("compute", 2, 0),
    ("join", 3, 0), ("corner", 3, 1), ("across", 3, 1), ("join", 2, 0),
    ("arrive", 1, 1), ("corner", 0, 1), ("compute", 3, 1), ("leave", 3, 0),
    ("first", 2, 0), ("join", 3, 1), ("corner", 1, 1), ("compute", 2, 1),
    ("compute", 0, 1), ("across", 1, 1), ("second", 2, 0), ("leave", 1, 0),
    ("leave", 3, 1), ("join", 2, 1), ("first", 2, 1), ("compute", 1, 1),
    ("first", 0, 0), ("join", 1, 1), ("leave", 2, 0), ("second", 2, 1),
    ("leave", 2, 1), ("second", 0, 0), ("leave", 1, 1), ("join", 0, 1),
    ("first", 0, 1), ("final", 0, 0), ("second", 0, 1), ("final", 0, 1),
)


def hand_over(first_in, second_in, first_out, second_out):
    first_out[...] = first_in[...]
    second_out[...] = second_in[...]


def layer(
    attn_out, out_weight, residual_in, gate_up, down, ids, filled, router, router_bias,
    out_bias, norm_gain, next_gain, bias_all, down_bias,
):
    tokens, features = attn_out.shape
    block_rows, width = residual_in.shape
    rows = block_rows // HALVES
    wide = -(-width // 128) * 128
    bf16, f32 = jnp.bfloat16, jnp.float32
    vmem = pl.BlockSpec(memory_space=pltpu.VMEM)
    smem = pl.BlockSpec(memory_space=pltpu.SMEM)
    anywhere = pl.BlockSpec(memory_space=pl.ANY)
    attn = attn_out.reshape(4, 2, block_rows, features)
    out_rows = out_weight.T
    dma = pltpu.SemaphoreType.DMA
    results = pl.pallas_call(
        layer_kernel,
        out_shape=[jax.ShapeDtypeStruct((block_rows, width), bf16)] * 2,
        in_specs=[anywhere] * 5 + [vmem, smem, vmem, smem] + [vmem] * 5,
        out_specs=[vmem, vmem],
        scratch_shapes=[
            pltpu.VMEM(attn.shape, bf16),
            pltpu.VMEM(out_rows.shape, bf16),
            pltpu.VMEM(residual_in.shape, bf16),
            pltpu.VMEM(gate_up.shape, bf16),
            pltpu.VMEM(down.shape, bf16),
            dma((5,)),
            pltpu.VMEM((128, width), bf16),
            pltpu.VMEM(gate_up.shape[:2], f32),
            pltpu.VMEM((block_rows, 128), f32),
            pltpu.VMEM((block_rows, width), f32),
            pltpu.VMEM((HALVES, 2, 2, 2, rows, width), bf16),
            pltpu.VMEM((HALVES, 2, 2, rows, width), bf16),
            pltpu.VMEM((HALVES, 2, rows // 2, width), bf16),
            pltpu.VMEM((HALVES, 2, rows // 2, width), bf16),
            pltpu.VMEM((HALVES, rows, width), bf16),
            dma((HALVES, 5)),
            dma((HALVES, 5)),
            pltpu.VMEM((4, HALVES, 8, rows, wide), bf16),
            dma((4, HALVES, 9)),
            dma((4, HALVES, 9)),
            pltpu.VMEM((4, HALVES, 2, 2, 2, rows, width), bf16),
            pltpu.VMEM((4, HALVES, 2, 2, rows, width), bf16),
            pltpu.VMEM((2, HALVES, 2, rows // 2, width), bf16),
            pltpu.VMEM((2, HALVES, 2, rows // 2, width), bf16),
            pltpu.VMEM((2, HALVES, rows, width), bf16),
            pltpu.VMEM((2, HALVES, rows, width), bf16),
            pltpu.VMEM((2, HALVES, rows, width), bf16),
            pltpu.VMEM((2, HALVES, rows, width), bf16),
            pltpu.VMEM((3, HALVES, rows, width), bf16),
            pltpu.VMEM((3, HALVES, rows, width), bf16),
            dma((4, HALVES, 6)),
            dma((4, HALVES, 6)),
        ],
        compiler_params=pltpu.CompilerParams(
            collective_id=0, has_side_effects=True, vmem_limit_bytes=60 * 1024 * 1024
        ),
    )(
        attn, out_rows, residual_in, gate_up, down, ids, filled, router, router_bias,
        out_bias, norm_gain, next_gain, bias_all, down_bias,
    )
    return pl.pallas_call(
        hand_over,
        out_shape=[jax.ShapeDtypeStruct((block_rows, width), bf16)] * 2,
        in_specs=[vmem] * 2,
        out_specs=[vmem] * 2,
    )(*results)


def dense_body(
    attn_out,
    out_weight,
    out_bias,
    residual_in,
    norm_gain,
    router_weight,
    router_bias,
    expert_ids,
    filled_rows,
    gate_up,
    gate_up_bias,
    down_weight,
    down_bias,
    next_gain,
):
    return tuple(
        layer(
            attn_out, out_weight, residual_in, gate_up[0], down_weight[0], expert_ids.T,
            filled_rows, router_weight.T, router_bias, out_bias, norm_gain,
            next_gain, gate_up_bias[0], down_bias,
        )
    )


def body(*arrays):
    residual_in, gate_up, down_weight = arrays[3], arrays[9], arrays[11]
    dp_size, expert_size = lax.axis_size("dp"), lax.axis_size("expert")
    token_rows = residual_in.shape[0] * dp_size * expert_size
    weight_rows = dp_size * (2 * gate_up.shape[2] + down_weight.shape[1])
    if gate_up.shape[0] == 1 and expert_size == 8 and dp_size == 4 and 2 * token_rows <= weight_rows:
        return dense_body(*arrays)
    return routed_body(*arrays)


def solution(mesh):
    return jax.shard_map(
        body,
        mesh=mesh,
        in_specs=(
            P("dp", "expert"),
            P("expert", None),
            P(),
            P(("dp", "expert"), None),
            P(),
            P(),
            P(),
            P(("dp", "expert"), None),
            P(("dp", "expert")),
            P("expert", None, "dp", None),
            P("expert", None, None),
            P("expert", "dp", None),
            P("expert", None),
            P(),
        ),
        out_specs=(P(("dp", "expert"), None), P(("dp", "expert"), None)),
        check_vma=False,
    )
```
